256 devices in a mesh: dp: 32 (over z_hi, x, y), tensor: 8 (over z_lo, core).
Axes of the slice: x: 4, y: 4, z: 8 (z_hi: 2, z_lo: 4; z = z_hi * 4 + z_lo), core: 2. Of those that a mesh axis runs over, the one named last changes fastest.
Arguments:
- activations: bfloat16 [8192, 53248], P('dp', 'tensor'), may hold values from -32 to 32
- test_matrix: bfloat16 [53248, 256], P('tensor', 'dp'), may hold values from -0.02734375 to 0.02734375
- gradient: bfloat16 [53248, 8192], P('tensor', 'dp'), may hold values from -16 to 16
Outputs:
- preconditioned: bfloat16 [53248, 8192], P('tensor', 'dp')
- gram_matrix: float32 [256, 256], replicated
The draws below stay inside these ranges and needn't reach their ends.
All inputs are finite; a program needn't handle non-finite values.
Results may differ from the reference program's by a relative error of at most 0.0034.
Values may be sent and summed in bfloat16 or wider, within the bound.
A program may use at most 128 MiB of HBM per device.

```python
import math
import jax
import jax.numpy as jnp
from jax import lax

INNER_WIDTH = 53248
GRAD_COLS = 8192
SKETCH_RANK = 256
TOKENS = 8192


def feature_scales(key):
    scale_key = jax.random.fold_in(key, 9173)
    return jnp.exp(jax.random.uniform(scale_key, (INNER_WIDTH,), jnp.float32, 0.0, math.log(10.0)))


def draw_activations(key, part):
    scales = feature_scales(key)
    base_key = jax.random.fold_in(key, 11)
    row_key = jax.random.fold_in(key, 12)
    position = jnp.arange(TOKENS, dtype=jnp.float32) / max(TOKENS - 1, 1)
    row_scale = jnp.exp(position * math.log(3.0) + jax.random.uniform(row_key, (TOKENS,), jnp.float32, 0.0, math.log(3.0)))
    values = jax.random.normal(base_key, (TOKENS, INNER_WIDTH), jnp.float32)
    values = values * row_scale[:, None] * scales[None, :] / 8.0
    return jnp.clip(values, -32.0, 32.0).astype(jnp.bfloat16)


def draw_gradient(key, part):
    scales = feature_scales(key)
    base_key = jax.random.fold_in(key, 21)
    values = jax.random.normal(base_key, (INNER_WIDTH, GRAD_COLS), jnp.float32)
    values = values * scales[:, None] / 2.0
    return jnp.clip(values, -16.0, 16.0).astype(jnp.bfloat16)


def block_scale(own_key, extent, cuts, least, top_value):
    def one(dim, blocks):
        draws = jax.random.uniform(jax.random.fold_in(jax.random.fold_in(own_key, 6), dim), (blocks,), jnp.float32, least / len(cuts), top_value / len(cuts))
        return jnp.repeat(jnp.exp(draws), extent[dim] // blocks).reshape((-1,) + (1,) * (len(extent) - dim - 1))

    level = one(*cuts[0])
    for cut in cuts[1:]:
        level = level * one(*cut)
    return level


def gaussian(key, shape, scale, limit, shards=(), kind=jnp.bfloat16):
    entries = jax.random.normal(key, shape, jnp.float32) * scale
    if len(shards) > 0:
        entries = block_scale(key, shape, shards, -0.22, 0.18) * entries
    return jnp.clip(entries, min=-limit, max=limit).astype(kind)


def setup_inputs(seed: int = 0) -> dict:
    arg_keys = jax.random.split(jax.random.key(seed), 4)
    return {
        "activations": draw_activations(jax.random.fold_in(arg_keys[3], 71), 0),
        "test_matrix": gaussian(arg_keys[1], (INNER_WIDTH, SKETCH_RANK), INNER_WIDTH ** -0.5, 0.02734375, ((0, 8), (1, 32))),
        "gradient": draw_gradient(jax.random.fold_in(arg_keys[3], 71), 0),
    }


damping_ratio = 0.1

def symmetric(matrix):
    return 0.5 * (matrix + matrix.T)

def reference(activations, test_matrix, gradient):
    tokens = activations.shape[0]
    sketch = jnp.dot(activations.astype(jnp.float32), test_matrix.astype(jnp.float32), preferred_element_type=jnp.float32)
    sketch_low = sketch.astype(jnp.bfloat16)
    factor = lax.dot_general(activations.astype(jnp.float32), sketch_low.astype(jnp.float32), (((0,), (0,)), ((), ())), preferred_element_type=jnp.float32) / tokens
    core_matrix = symmetric(jnp.dot(test_matrix.astype(jnp.float32).T, factor, precision=lax.Precision.HIGHEST))
    chol_lower = jnp.linalg.cholesky(core_matrix)
    basis_full = jax.scipy.linalg.solve_triangular(chol_lower, factor.T, lower=True).T
    gram_matrix = jnp.dot(basis_full.T, basis_full, precision=lax.Precision.HIGHEST)
    damping = damping_ratio * jnp.trace(gram_matrix) / SKETCH_RANK
    kernel_lower = jnp.linalg.cholesky(gram_matrix + damping * jnp.eye(SKETCH_RANK, dtype=jnp.float32))
    basis_low = basis_full.astype(jnp.bfloat16)
    projected = lax.dot_general(basis_low.astype(jnp.float32), gradient.astype(jnp.float32), (((0,), (0,)), ((), ())), preferred_element_type=jnp.float32)
    weights = jax.scipy.linalg.cho_solve((kernel_lower, True), projected).astype(jnp.bfloat16)
    correction = jnp.dot(basis_low.astype(jnp.float32), weights.astype(jnp.float32), preferred_element_type=jnp.float32)
    return ((gradient.astype(jnp.float32) - correction).astype(jnp.bfloat16), gram_matrix)
```

```python
import jax
import jax.numpy as jnp
from jax import lax
from jax.experimental import pallas as pl
from jax.experimental.pallas import tpu as pltpu
from jax.sharding import PartitionSpec as P

damping_ratio = 0.1
MESH = pl.DeviceIdType.MESH
F32, BF16 = jnp.float32, jnp.bfloat16
HI = lax.Precision.HIGHEST
ZN, XN, YN, TN = 2, 4, 4, 8
NB = 32
SEMS = 160


def dot(a, b, ca, cb, precision=None):
    return lax.dot_general(
        a, b, (((ca,), (cb,)), ((), ())), precision=precision, preferred_element_type=F32
    )


def mod(a, n):
    return lax.rem(a, n)


class Net:
    def __init__(self, send_sem, recv_sem):
        dp, self.t = lax.axis_index("dp"), lax.axis_index("tensor")
        self.z, self.x, self.y = lax.div(dp, XN * YN), mod(lax.div(dp, YN), XN), mod(dp, YN)
        self.send_sem, self.recv_sem, self.count, self.sent = send_sem, recv_sem, 0, []

    def dp(self, z=None, x=None, y=None):
        z, x, y = (own if v is None else v for v, own in ((z, self.z), (x, self.x), (y, self.y)))
        return {"dp": (z * XN + x) * YN + y}

    def step(self, axis, by):
        own, n = (self.x, XN) if axis == "x" else (self.y, YN)
        return self.dp(**{axis: mod(own + by + n, n)})

    def send(self, src, dst, device):
        k = self.count
        self.count += 1
        copy = pltpu.make_async_remote_copy(
            src_ref=src,
            dst_ref=dst,
            send_sem=self.send_sem.at[k],
            recv_sem=self.recv_sem.at[k],
            device_id=device,
            device_id_type=MESH,
        )
        copy.start()
        self.sent.append(copy)
        return copy

    def finish(self):
        for copy in self.sent:
            copy.wait_send()


def barrier(net):
    sem = pltpu.get_barrier_semaphore()
    peers = [{"tensor": mod(net.t + o, TN)} for o in range(1, TN)]
    peers += [net.step("x", o) for o in range(1, XN)] + [net.step("y", o) for o in range(1, YN)]
    peers += [net.dp(z=1 - net.z)]
    for peer in peers:
        pl.semaphore_signal(sem, inc=1, device_id=peer, device_id_type=MESH)
    pl.semaphore_wait(sem, len(peers))


def gather(net, buf):
    half = buf.shape[-1] // 2
    order = (("x", "y"), ("y", "x"))
    z, other = net.z, 1 - net.z
    place = {"x": net.x, "y": net.y}

    def first(h, plane, by):
        a = order[h][0]
        i = mod(place[a] + by + 4, 4)
        lanes = pl.ds(h * half, half)
        return buf.at[plane, i, net.y, :, lanes] if a == "x" else buf.at[plane, net.x, i, :, lanes]

    def second(h, plane, by):
        a = order[h][1]
        i = mod(place[a] + by + 4, 4)
        lanes = pl.ds(h * half, half)
        return buf.at[plane, i, :, :, lanes] if a == "x" else buf.at[plane, :, i, :, lanes]

    def both(part, h, ph, plane):
        a = order[h][ph]
        ref = part(h, plane, 0)
        return net.send(ref, ref, net.step(a, 1)), net.send(ref, ref, net.step(a, -1))

    def on(part, h, ph, plane, by):
        ref = part(h, plane, -by)
        return net.send(ref, ref, net.step(order[h][ph], by))

    own = buf.at[z, net.x, net.y]
    pair = net.send(own, own, net.dp(z=other))
    e1 = [both(first, h, 0, z) for h in (0, 1)]
    yield
    f1 = []
    for h in (0, 1):
        e1[h][0].wait_recv()
        f1.append(on(first, h, 0, z, 1))
    for h in (0, 1):
        e1[h][1].wait_recv()
    yield
    pair.wait_recv()
    l1 = [both(first, h, 0, other) for h in (0, 1)]
    e2 = []
    for h in (0, 1):
        f1[h].wait_recv()
        e2.append(both(second, h, 1, z))
    yield
    g1 = []
    for h in (0, 1):
        l1[h][1].wait_recv()
        g1.append(on(first, h, 0, other, -1))
        l1[h][0].wait_recv()
    yield
    l2 = []
    for h in (0, 1):
        g1[h].wait_recv()
        l2.append(both(second, h, 1, other))
    yield
    f2 = []
    for h in (0, 1):
        e2[h][0].wait_recv()
        f2.append(on(second, h, 1, z, 1))
    yield
    g2 = []
    for h in (0, 1):
        l2[h][1].wait_recv()
        g2.append(on(second, h, 1, other, -1))
    yield
    for h in (0, 1):
        e2[h][1].wait_recv()
        f2[h].wait_recv()
        l2[h][0].wait_recv()
        g2[h].wait_recv()
    yield


def add(*refs):
    total = refs[0][...].astype(F32)
    for ref in refs[1:]:
        total = total + ref[...].astype(F32)
    return total


def scatter(net, part, bufs, out):
    order = (("x", "y"), ("y", "x"))
    place = {"x": net.x, "y": net.y}
    half = part.shape[-1] // 2

    def first(h, plane, by):
        a = order[h][0]
        i = mod(place[a] + by + 4, 4)
        lanes = pl.ds(h * half, half)
        return part.at[plane, i, :, :, lanes] if a == "x" else part.at[plane, :, i, :, lanes]

    def second(h, plane, by):
        a = order[h][1]
        i = mod(place[a] + by + 4, 4)
        lanes = pl.ds(h * half, half)
        return part.at[plane, i, net.y, :, lanes] if a == "x" else part.at[plane, net.x, i, :, lanes]

    for ph, block in ((0, first), (1, second)):
        near, far = bufs[2 * ph], bufs[2 * ph + 1]
        s1, s2 = [], []
        for h in (0, 1):
            up, down = net.step(order[h][ph], 1), net.step(order[h][ph], -1)
            s1.append(
                (
                    net.send(block(h, 0, 2), far.at[h, 0], up),
                    net.send(block(h, 1, 2), far.at[h, 1], down),
                )
            )
        for h in (0, 1):
            up, down = net.step(order[h][ph], 1), net.step(order[h][ph], -1)
            s2.append(
                [
                    net.send(block(h, 1, 1), near.at[h, 0, 1], up),
                    net.send(block(h, 0, -1), near.at[h, 1, 0], down),
                ]
            )
        yield
        for h in (0, 1):
            up, down = net.step(order[h][ph], 1), net.step(order[h][ph], -1)
            s1[h][0].wait_recv()
            ref = block(h, 0, 1)
            ref[...] = add(ref, far.at[h, 0]).astype(BF16)
            s2[h].append(net.send(ref, near.at[h, 0, 0], up))
            s1[h][1].wait_recv()
            ref = block(h, 1, -1)
            ref[...] = add(ref, far.at[h, 1]).astype(BF16)
            s2[h].append(net.send(ref, near.at[h, 1, 1], down))
        yield
        for h in (0, 1):
            for copy in s2[h]:
                copy.wait_recv()
            for plane in (0, 1):
                ref = block(h, plane, 0)
                ref[...] = add(ref, near.at[h, 0, plane], near.at[h, 1, plane]).astype(BF16)
    got = bufs[4]
    last = net.send(part.at[1 - net.z, net.x, net.y], got, net.dp(z=1 - net.z))
    yield
    last.wait_recv()
    out[...] = add(part.at[net.z, net.x, net.y], got)
    yield


def spread(net, part, got):
    copies = []
    for o in range(1, TN):
        peer = mod(net.t + o, TN)
        copies.append(net.send(part.at[peer], got.at[net.t], {"tensor": peer}))
    got[net.t] = part[net.t]
    return copies


def share(net, buf):
    own = buf.at[net.t]
    return [net.send(own, own, {"tensor": mod(net.t + o, TN)}) for o in range(1, TN)]


def landed(copies):
    for copy in copies:
        copy.wait_recv()


def slots(ref):
    total = ref[0]
    for i in range(1, ref.shape[0]):
        total = total + ref[i]
    return total


def total_sum(net, part, got, gy, gx, gz, res):
    copies = spread(net, part, got)
    yield
    landed(copies)
    gy[net.y] = slots(got)
    copies = [net.send(gy.at[net.y], gy.at[net.y], net.step("y", o)) for o in range(1, YN)]
    yield
    landed(copies)
    gx[net.x] = slots(gy)
    copies = [net.send(gx.at[net.x], gx.at[net.x], net.step("x", o)) for o in range(1, XN)]
    yield
    landed(copies)
    gz[net.z] = slots(gx)
    copy = net.send(gz.at[net.z], gz.at[net.z], net.dp(z=1 - net.z))
    yield
    copy.wait_recv()
    res[net.t] = slots(gz)
    copies = share(net, res)
    yield
    landed(copies)
    yield


def start_factor(work, matrix):
    n = matrix.shape[0]
    row = lax.broadcasted_iota(jnp.int32, (n, n), 0)
    col = lax.broadcasted_iota(jnp.int32, (n, n), 1)
    work[:, :n] = matrix
    work[:, n:] = (row == col).astype(F32)


def factor_panels(work, inverse, low, high):
    n = inverse.shape[0]

    def panel(p, carry):
        r0 = pl.multiple_of(p * NB, NB)
        rows = work[pl.ds(r0, NB), :]
        turned = pltpu.roll(rows[:, :n], mod(n - p * NB, n), 1)[:, :128]
        row = lax.broadcasted_iota(jnp.int32, (NB, 128), 0)
        lane = lax.broadcasted_iota(jnp.int32, (NB, 128), 1)
        block = jnp.where(lane < NB, turned, (lane - NB == row).astype(F32))
        for k in range(NB - 1):
            scale = block[:, k : k + 1] * (1.0 / block[k : k + 1, k : k + 1])
            scale = jnp.where(row[:, :1] > k, scale, 0.0)
            block = block - scale * block[k : k + 1, :]
        pivots = jnp.sum(jnp.where(lane == row, block, 0.0), axis=1, keepdims=True)
        block = block / jnp.sqrt(pivots)
        small = block[:, NB : 2 * NB]
        done = dot(small, rows, 1, 0, HI)
        inverse[pl.ds(r0, NB), :] = done[:, n:]
        ahead = lax.broadcasted_iota(jnp.int32, (NB, n), 1) >= r0 + NB
        upper = jnp.where(ahead, done[:, :n], 0.0)
        work[...] = work[...] - dot(upper.T, done, 1, 0, HI)
        return carry

    lax.fori_loop(low, high, panel, 0)


def factor_steps(work, inverse, cuts):
    for low, high in zip(cuts[:-1], cuts[1:]):
        factor_panels(work, inverse, low, high)
        yield


def together(*tasks):
    tasks = list(tasks)
    while tasks:
        for task in list(tasks):
            try:
                next(task)
            except StopIteration:
                tasks.remove(task)


def chain(*tasks):
    for task in tasks:
        if callable(task):
            task()
            continue
        yield from task


def kernel(
    om_hbm, a_hbm, g_hbm,
    basis_hbm, wt_out, gram_out,
    om, a, g, part, basis, factor,
    near1, far1, near2, far2, pair,
    ypart, ygot, ylow,
    cpart, cgot, cy, cx, cz, core,
    gpart, ggot, gy, gx, gz, gram,
    ppart, pgot, wt,
    work, linv, kinv,
    send_sem, recv_sem, load_sem,
):
    net = Net(send_sem, recv_sem)
    hidden, rank = basis_hbm.shape[0] * basis_hbm.shape[1] * basis_hbm.shape[2] * basis_hbm.shape[3], basis_hbm.shape[4]
    tokens = a.shape[0] * ZN * XN * YN
    load_om = pltpu.make_async_copy(om_hbm, om.at[net.z, net.x, net.y], load_sem.at[0])
    load_a = pltpu.make_async_copy(a_hbm, a, load_sem.at[1])
    load_g = pltpu.make_async_copy(g_hbm, g, load_sem.at[2])
    load_om.start()
    load_a.start()
    load_g.start()
    barrier(net)
    load_om.wait()
    together(gather(net, om))
    load_a.wait()

    ck = 512
    ypart[...] = jnp.zeros_like(ypart)

    def sketch(i, carry):
        lanes = pl.ds(pl.multiple_of(i * ck, ck), ck)
        probe = om[:, :, :, :, lanes].astype(F32).reshape(rank, ck).astype(BF16)
        ypart[...] += dot(a[:, lanes], probe, 1, 1).reshape(ypart.shape)
        return carry

    lax.fori_loop(0, hidden // ck, sketch, 0)
    landed(spread(net, ypart, ygot))
    yrows = slots(ygot)
    ylow[net.t] = yrows.astype(BF16)
    copies = share(net, ylow)
    cpart[...] = (
        dot(yrows, yrows.astype(BF16).astype(F32), 0, 0, HI) * (1.0 / tokens)
    ).reshape(cpart.shape)
    core_task = total_sum(net, cpart, cgot, cy, cx, cz, core)
    next(core_task)
    landed(copies)
    low = ylow[...].reshape(a.shape[0], rank)

    wide = hidden // 4
    per = wide // part.shape[3]
    for c in range(4):
        block = dot(a[:, c * wide : (c + 1) * wide], low, 0, 0).astype(BF16)
        part[c // 2, (c % 2) * 2 : (c % 2) * 2 + 2] = block.reshape((per // YN, YN) + part.shape[3:])

    def start_core():
        full = core[...].reshape(rank, rank)
        start_factor(work, 0.5 * (full + full.T))

    panels = rank // NB
    cuts = list(range(0, panels + 1, 2))
    together(
        scatter(net, part, (near1, far1, near2, far2, pair), factor),
        chain(core_task, start_core, factor_steps(work, linv, cuts)),
    )
    local = dot(factor[...] * (1.0 / tokens), linv[...], 1, 1, HI)
    basis[net.z, net.x, net.y] = local.astype(BF16)

    basis_task = gather(net, basis)
    next(basis_task)
    gpart[...] = dot(local, local, 0, 0, HI).reshape(gpart.shape)

    def start_gram():
        full = gram[...].reshape(rank, rank)
        gram_out[...] = full
        row = lax.broadcasted_iota(jnp.int32, (rank, rank), 0)
        col = lax.broadcasted_iota(jnp.int32, (rank, rank), 1)
        eye = (row == col).astype(F32)
        damping = (damping_ratio / rank) * jnp.sum(jnp.sum(full * eye, axis=1, keepdims=True), axis=0, keepdims=True)
        start_factor(work, full + damping * eye)

    together(
        basis_task,
        chain(total_sum(net, gpart, ggot, gy, gx, gz, gram), start_gram, factor_steps(work, kinv, cuts)),
    )
    store = pltpu.make_async_copy(basis, basis_hbm, load_sem.at[3])
    store.start()
    load_g.wait()
    ppart[...] = jnp.zeros_like(ppart)
    rows = basis.shape[3]

    for c in range(4):
        wide_rows = pl.ds(c * wide, wide)
        block = basis[c // 2, (c % 2) * 2 : (c % 2) * 2 + 2].reshape(wide, rank)
        ppart[...] += dot(g[wide_rows, :], block, 0, 0).reshape(ppart.shape)
    landed(spread(net, ppart, pgot))
    solved = dot(dot(slots(pgot), kinv[...], 1, 1, HI), kinv[...], 1, 0, HI)
    wt[net.t] = solved.astype(BF16)
    landed(share(net, wt))
    wt_out[...] = wt[...].reshape(wt_out.shape)
    store.wait()
    net.finish()


def local(activations, test_matrix, gradient):
    tok, hidden = activations.shape
    cols = gradient.shape[1]
    dp = lax.axis_size("dp")
    probe = test_matrix.T
    share_cols = probe.shape[0]
    rank = share_cols * dp
    rows = hidden // dp
    own = rank // TN
    vm, dma = pltpu.VMEM, pltpu.SemaphoreType.DMA
    small = [vm((TN, own, rank), F32), vm((TN, own, rank), F32)]
    sums = small + [vm((YN, own, rank), F32), vm((XN, own, rank), F32), vm((ZN, own, rank), F32), vm((TN, own, rank), F32)]
    basis, wt, gram = pl.pallas_call(
        kernel,
        out_shape=(
            jax.ShapeDtypeStruct((ZN, XN, YN, rows, rank), BF16),
            jax.ShapeDtypeStruct((cols, rank), BF16),
            jax.ShapeDtypeStruct((rank, rank), F32),
        ),
        in_specs=[pl.BlockSpec(memory_space=pl.ANY)] * 3,
        out_specs=(
            pl.BlockSpec(memory_space=pl.ANY),
            pl.BlockSpec(memory_space=pltpu.VMEM),
            pl.BlockSpec(memory_space=pltpu.VMEM),
        ),
        scratch_shapes=[
            vm((ZN, XN, YN, share_cols, hidden), BF16),
            vm((tok, hidden), BF16),
            vm((hidden, cols), BF16),
            vm((ZN, XN, YN, rows, rank), BF16),
            vm((ZN, XN, YN, rows, rank), BF16),
            vm((rows, rank), F32),
            vm((2, 2, 2, 4, rows, rank // 2), BF16),
            vm((2, 2, 4, rows, rank // 2), BF16),
            vm((2, 2, 2, rows, rank // 2), BF16),
            vm((2, 2, rows, rank // 2), BF16),
            vm((rows, rank), BF16),
        ]
        + small
        + [vm((TN, own, rank), BF16)]
        + sums
        + sums
        + small
        + [
            vm((TN, own, rank), BF16),
            vm((rank, 2 * rank), F32),
            vm((rank, rank), F32),
            vm((rank, rank), F32),
            dma((SEMS,)),
            dma((SEMS,)),
            dma((4,)),
        ],
        compiler_params=pltpu.CompilerParams(
            collective_id=0, has_side_effects=True, vmem_limit_bytes=60 << 20
        ),
    )(probe, activations, gradient)
    correction = lax.dot_general(
        basis.reshape(hidden, rank), wt, (((1,), (1,)), ((), ())), preferred_element_type=F32
    )
    return (gradient.astype(F32) - correction).astype(BF16), gram


def solution(mesh):
    placed = (P("dp", "tensor"), P("tensor", "dp"), P("tensor", "dp"))
    return jax.shard_map(
        local, mesh=mesh, in_specs=placed, out_specs=(P("tensor", "dp"), P()), check_vma=False
    )
```

```python
import jax
import jax.numpy as jnp
from jax import lax
from jax.experimental import pallas as pl
from jax.experimental.pallas import tpu as pltpu
from jax.sharding import PartitionSpec as P

damping_ratio = 0.1
MESH = pl.DeviceIdType.MESH
F32, BF16 = jnp.float32, jnp.bfloat16
HI = lax.Precision.HIGHEST
ZN, XN, YN, TN = 2, 4, 4, 8
NB = 32
AHEAD = 6
SEMS = 210


def dot(a, b, ca, cb, precision=None):
    return lax.dot_general(
        a, b, (((ca,), (cb,)), ((), ())), precision=precision, preferred_element_type=F32
    )


def mod(a, n):
    return lax.rem(a, n)


class Net:
    def __init__(self, send_sem, recv_sem):
        dp, self.t = lax.axis_index("dp"), lax.axis_index("tensor")
        self.z, self.x, self.y = lax.div(dp, XN * YN), mod(lax.div(dp, YN), XN), mod(dp, YN)
        self.send_sem, self.recv_sem, self.count, self.sent = send_sem, recv_sem, 0, []

    def dp(self, z=None, x=None, y=None):
        z, x, y = (own if v is None else v for v, own in ((z, self.z), (x, self.x), (y, self.y)))
        return {"dp": (z * XN + x) * YN + y}

    def step(self, axis, by):
        own, n = (self.x, XN) if axis == "x" else (self.y, YN)
        return self.dp(**{axis: mod(own + by + n, n)})

    def send(self, src, dst, device):
        k = self.count
        self.count += 1
        copy = pltpu.make_async_remote_copy(
            src_ref=src,
            dst_ref=dst,
            send_sem=self.send_sem.at[k],
            recv_sem=self.recv_sem.at[k],
            device_id=device,
            device_id_type=MESH,
        )
        copy.start()
        self.sent.append(copy)
        return copy

    def finish(self):
        assert self.count == SEMS, self.count
        for copy in self.sent:
            copy.wait_send()


def barrier(net):
    sem = pltpu.get_barrier_semaphore()
    peers = [{"tensor": mod(net.t + o, TN)} for o in range(1, TN)]
    peers += [net.step("x", o) for o in range(1, XN)] + [net.step("y", o) for o in range(1, YN)]
    peers += [net.dp(z=1 - net.z)]
    for peer in peers:
        pl.semaphore_signal(sem, inc=1, device_id=peer, device_id_type=MESH)
    pl.semaphore_wait(sem, len(peers))


def gather(net, buf):
    half = buf.shape[-1] // 2
    order = (("x", "y"), ("y", "x"))
    planes = (net.z, 1 - net.z)
    place = {"x": net.x, "y": net.y}
    halves = (0, 1)

    def move(h, ph, plane, i, j, by):
        at = {order[h][0]: mod(place[order[h][0]] + i + 4, 4), order[h][1]: mod(place[order[h][1]] + j + 4, 4)}
        ref = buf.at[planes[plane], at["x"], at["y"], :, pl.ds(h * half, half)]
        return net.send(ref, ref, net.step(order[h][ph], by))

    def both(h, ph, plane, i):
        return move(h, ph, plane, i, 0, 1), move(h, ph, plane, i, 0, -1)

    one = [[None, None], [None, None]]
    two = [[{}, {}], [{}, {}]]
    hop = [[None, None], [None, None]]
    hops = []
    side = (0, 1)

    def launch(plane):
        for h in halves:
            one[plane][h] = both(h, 0, plane, 0)
        for h in halves:
            two[plane][h][0] = both(h, 1, plane, 0)

    def near(plane):
        by = 1 if plane == 0 else -1
        for h in halves:
            for d in (side[plane], 1 - side[plane]):
                one[plane][h][d].wait_recv()
                i = -1 if d == 0 else 1
                if d == side[plane]:
                    hop[plane][h] = move(h, 0, plane, -by, 0, by)
                two[plane][h][i] = both(h, 1, plane, i)

    def far(plane):
        for h in halves:
            hop[plane][h].wait_recv()
            two[plane][h][2] = both(h, 1, plane, 2)

    def onward(plane, i):
        by = 1 if plane == 0 else -1
        for h in halves:
            two[plane][h][i][side[plane]].wait_recv()
            hops.append(move(h, 1, plane, i, -by, by))

    own = buf.at[net.z, net.x, net.y]
    pair = net.send(own, own, net.dp(z=1 - net.z))
    launch(0)
    yield
    near(0)
    yield
    onward(0, 0)
    far(0)
    pair.wait_recv()
    launch(1)
    yield
    onward(0, -1)
    onward(0, 1)
    yield
    near(1)
    onward(0, 2)
    yield
    onward(1, 0)
    far(1)
    yield
    onward(1, -1)
    onward(1, 1)
    yield
    onward(1, 2)
    yield
    for plane in (0, 1):
        for h in halves:
            for i in (0, -1, 1, 2):
                two[plane][h][i][1 - side[plane]].wait_recv()
    for copy in hops:
        copy.wait_recv()
    yield


def add(*refs):
    total = refs[0][...].astype(F32)
    for ref in refs[1:]:
        total = total + ref[...].astype(F32)
    return total


def scatter(net, part, bufs, out, scale):
    order = (("x", "y"), ("y", "x"))
    place = {"x": net.x, "y": net.y}
    half = part.shape[-1] // 2

    def first(h, plane, by):
        a = order[h][0]
        i = mod(place[a] + by + 4, 4)
        lanes = pl.ds(h * half, half)
        return part.at[plane, i, :, :, lanes] if a == "x" else part.at[plane, :, i, :, lanes]

    def second(h, plane, by):
        a = order[h][1]
        i = mod(place[a] + by + 4, 4)
        lanes = pl.ds(h * half, half)
        return part.at[plane, i, net.y, :, lanes] if a == "x" else part.at[plane, net.x, i, :, lanes]

    for ph, block in ((0, first), (1, second)):
        near, far = bufs[2 * ph], bufs[2 * ph + 1]
        s1, s2 = [], []
        for h in (0, 1):
            up, down = net.step(order[h][ph], 1), net.step(order[h][ph], -1)
            s1.append(
                (
                    net.send(block(h, 0, 2), far.at[h, 0], up),
                    net.send(block(h, 1, 2), far.at[h, 1], down),
                )
            )
        yield
        for h in (0, 1):
            up, down = net.step(order[h][ph], 1), net.step(order[h][ph], -1)
            s2.append(
                [
                    net.send(block(h, 1, 1), near.at[h, 0, 1], up),
                    net.send(block(h, 0, -1), near.at[h, 1, 0], down),
                ]
            )
        yield
        for h in (0, 1):
            up, down = net.step(order[h][ph], 1), net.step(order[h][ph], -1)
            s1[h][0].wait_recv()
            ref = block(h, 0, 1)
            ref[...] = add(ref, far.at[h, 0]).astype(BF16)
            s2[h].append(net.send(ref, near.at[h, 0, 0], up))
            s1[h][1].wait_recv()
            ref = block(h, 1, -1)
            ref[...] = add(ref, far.at[h, 1]).astype(BF16)
            s2[h].append(net.send(ref, near.at[h, 1, 1], down))
        yield
        for h in (0, 1):
            for copy in s2[h]:
                copy.wait_recv()
            for plane in (0, 1):
                ref = block(h, plane, 0)
                ref[...] = add(ref, near.at[h, 0, plane], near.at[h, 1, plane]).astype(BF16)
    got = bufs[4]
    last = net.send(part.at[1 - net.z, net.x, net.y], got, net.dp(z=1 - net.z))
    yield
    last.wait_recv()
    out[...] = add(part.at[net.z, net.x, net.y], got) * scale
    yield


def spread(net, part, got):
    copies = []
    for o in range(1, TN):
        peer = mod(net.t + o, TN)
        copies.append(net.send(part.at[peer], got.at[net.t], {"tensor": peer}))
    got[net.t] = part[net.t]
    return copies


def share(net, buf):
    own = buf.at[net.t]
    return [net.send(own, own, {"tensor": mod(net.t + o, TN)}) for o in range(1, TN)]


def landed(copies):
    for copy in copies:
        copy.wait_recv()


def slots(ref):
    total = ref[0]
    for i in range(1, ref.shape[0]):
        total = total + ref[i]
    return total


def dp_sum(net, rows, gy, gx, gz, res):
    gy[net.y] = rows
    copies = [net.send(gy.at[net.y], gy.at[net.y], net.step("y", o)) for o in range(1, YN)]
    yield
    landed(copies)
    gx[net.x] = slots(gy)
    copies = [net.send(gx.at[net.x], gx.at[net.x], net.step("x", o)) for o in range(1, XN)]
    yield
    landed(copies)
    gz[net.z] = slots(gx)
    copy = net.send(gz.at[net.z], gz.at[net.z], net.dp(z=1 - net.z))
    yield
    copy.wait_recv()
    res[net.t] = slots(gz)
    copies = share(net, res)
    yield
    landed(copies)
    yield


def total_sum(net, part, got, gy, gx, gz, res):
    copies = spread(net, part, got)
    yield
    landed(copies)
    yield from dp_sum(net, slots(got), gy, gx, gz, res)


def factor_steps(matrix, work, late, made, inverse):
    n = inverse.shape[0]
    row = lax.broadcasted_iota(jnp.int32, (n, n), 0)
    col = lax.broadcasted_iota(jnp.int32, (n, n), 1)
    work[:, :n] = matrix()
    work[:, n:] = (row == col).astype(F32)
    late[...] = jnp.zeros_like(late)
    made[...] = jnp.zeros_like(made)

    def panel(p, carry):
        r0 = pl.multiple_of(p * NB, NB)
        rows = work[pl.ds(r0, NB), :]
        turned = pltpu.roll(rows[:, :n], mod(n - p * NB, n), 1)[:, :128]
        row = lax.broadcasted_iota(jnp.int32, (NB, 128), 0)
        lane = lax.broadcasted_iota(jnp.int32, (NB, 128), 1)
        block = jnp.where(lane < NB, turned, (lane - NB == row).astype(F32))
        work[...] = work[...] - dot(late[...], made[...], 1, 0, HI)
        columns = [jnp.broadcast_to(block[:, k : k + 1], block.shape) for k in range(AHEAD)]
        for k in range(NB - 1):
            if k + AHEAD < NB:
                columns.append(jnp.broadcast_to(block[:, k + AHEAD : k + AHEAD + 1], block.shape))
            column = columns.pop(0)
            scale = jnp.where(row > k, column * (1.0 / column[k : k + 1, :]), 0.0)
            columns = [later - scale * later[k : k + 1, :] for later in columns]
            block = block - scale * block[k : k + 1, :]
        pivots = jnp.sum(jnp.where(lane == row, block, 0.0), axis=1, keepdims=True)
        block = block / jnp.sqrt(pivots)
        done = dot(block[:, NB : 2 * NB], rows, 1, 0, HI)
        inverse[pl.ds(r0, NB), :] = done[:, n:]
        ahead = lax.broadcasted_iota(jnp.int32, (NB, n), 1) >= r0 + NB
        late[...] = jnp.where(ahead, done[:, :n], 0.0).T
        made[...] = done
        r1 = pl.multiple_of(mod(r0 + NB, n), NB)
        work[pl.ds(r1, NB), :] = work[pl.ds(r1, NB), :] - dot(late[pl.ds(r1, NB), :], done, 1, 0, HI)
        late[pl.ds(r1, NB), :] = jnp.zeros((NB, NB), F32)
        return carry

    for p in range(n // NB):
        lax.fori_loop(p, p + 1, panel, 0)
        yield


def play(order, **tasks):
    for name in order.split():
        next(tasks[name])


def kernel(
    om_hbm, a_hbm, g_hbm,
    basis_hbm, wt_out, gram_out,
    om, a, g, part, basis, factor,
    near1, far1, near2, far2, pair,
    ypart, ygot, ylow,
    cy, cx, cz, core,
    gpart, ggot, gy, gx, gz, gram,
    ppart, pgot, wt,
    work, late, made, linv, kinv,
    send_sem, recv_sem, load_sem,
):
    net = Net(send_sem, recv_sem)
    hidden, rank = basis_hbm.shape[0] * basis_hbm.shape[1] * basis_hbm.shape[2] * basis_hbm.shape[3], basis_hbm.shape[4]
    tok = a.shape[0]
    tokens = tok * ZN * XN * YN
    load_om = pltpu.make_async_copy(om_hbm, om.at[net.z, net.x, net.y], load_sem.at[0])
    load_a = pltpu.make_async_copy(a_hbm, a, load_sem.at[1])
    load_g = pltpu.make_async_copy(g_hbm, g, load_sem.at[2])
    load_om.start()
    load_a.start()
    load_g.start()
    barrier(net)
    load_om.wait()
    for _ in gather(net, om):
        pass
    load_a.wait()

    ck = 512
    ypart[...] = jnp.zeros_like(ypart)

    def sketch(i, carry):
        lanes = pl.ds(pl.multiple_of(i * ck, ck), ck)
        probe = om[:, :, :, :, lanes].astype(F32).reshape(rank, ck).astype(BF16)
        ypart[...] += dot(probe, a[:, lanes], 1, 1).reshape(ypart.shape)
        return carry

    lax.fori_loop(0, hidden // ck, sketch, 0)
    landed(spread(net, ypart, ygot))
    yrows = slots(ygot)
    ylow[net.t] = yrows.astype(BF16)
    landed(share(net, ylow))
    low = ylow[...].reshape(rank, tok)
    crows = dot(yrows, low.astype(F32), 1, 1, HI) * (1.0 / tokens)

    def symmetric_core():
        full = core[...].reshape(rank, rank)
        return 0.5 * (full + full.T)

    def core_chain():
        yield from dp_sum(net, crows, cy, cx, cz, core)
        yield from factor_steps(symmetric_core, work, late, made, linv)

    def gram_sum():
        rows = factor[...]
        gpart[...] = dot(rows, rows, 0, 0, HI).reshape(gpart.shape)
        yield from total_sum(net, gpart, ggot, gy, gx, gz, gram)

    def gram_chain():
        half = dot(linv[...], gram[...].reshape(rank, rank), 1, 0, HI)
        full = dot(half, linv[...], 1, 1, HI)
        gram_out[...] = full
        row = lax.broadcasted_iota(jnp.int32, (rank, rank), 0)
        col = lax.broadcasted_iota(jnp.int32, (rank, rank), 1)
        eye = (row == col).astype(F32)
        trace = jnp.sum(jnp.sum(full * eye, axis=1, keepdims=True), axis=0, keepdims=True)
        yield from factor_steps(lambda: full + (damping_ratio / rank) * trace * eye, work, late, made, kinv)

    core_task = core_chain()
    gram_task = gram_sum()
    wide = hidden // 4
    per = wide // part.shape[3]
    low_t = low.T
    next(core_task)
    for c in range(4):
        block = dot(a[:, c * wide : (c + 1) * wide], low_t, 0, 0).astype(BF16)
        part[c // 2, (c % 2) * 2 : (c % 2) * 2 + 2] = block.reshape((per // YN, YN) + part.shape[3:])
    play(
        "r c r r c c r r c r c c c r c c c c r g c",
        c=core_task,
        r=scatter(net, part, (near1, far1, near2, far2, pair), factor, 1.0 / tokens),
        g=gram_task,
    )
    local = dot(factor[...], linv[...], 1, 1, HI)
    basis[net.z, net.x, net.y] = local.astype(BF16)
    kernel_task = gram_chain()
    play("b b g b g b g b b g b b b", b=gather(net, basis), g=gram_task)
    store = pltpu.make_async_copy(basis, basis_hbm, load_sem.at[3])
    store.start()
    load_g.wait()
    ppart[...] = jnp.zeros_like(ppart)
    for c in range(4):
        block = basis[c // 2, (c % 2) * 2 : (c % 2) * 2 + 2].reshape(wide, rank)
        ppart[...] += dot(g[c * wide : (c + 1) * wide, :], block, 0, 0).reshape(ppart.shape)
    copies = spread(net, ppart, pgot)
    play("g k k k k k k k k", g=gram_task, k=kernel_task)
    landed(copies)
    solved = dot(dot(slots(pgot), kinv[...], 1, 1, HI), kinv[...], 1, 0, HI)
    wt[net.t] = solved.astype(BF16)
    landed(share(net, wt))
    wt_out[...] = wt[...].reshape(wt_out.shape)
    store.wait()
    net.finish()


def local(activations, test_matrix, gradient):
    tok, hidden = activations.shape
    cols = gradient.shape[1]
    dp = lax.axis_size("dp")
    probe = test_matrix.T
    share_cols = probe.shape[0]
    rank = share_cols * dp
    rows = hidden // dp
    own = rank // TN
    vm, dma = pltpu.VMEM, pltpu.SemaphoreType.DMA
    small = [vm((TN, own, rank), F32), vm((TN, own, rank), F32)]
    dp_sums = [vm((n, own, rank), F32) for n in (YN, XN, ZN, TN)]
    basis, wt, gram = pl.pallas_call(
        kernel,
        out_shape=(
            jax.ShapeDtypeStruct((ZN, XN, YN, rows, rank), BF16),
            jax.ShapeDtypeStruct((cols, rank), BF16),
            jax.ShapeDtypeStruct((rank, rank), F32),
        ),
        in_specs=[pl.BlockSpec(memory_space=pl.ANY)] * 3,
        out_specs=(
            pl.BlockSpec(memory_space=pl.ANY),
            pl.BlockSpec(memory_space=pltpu.VMEM),
            pl.BlockSpec(memory_space=pltpu.VMEM),
        ),
        scratch_shapes=[
            vm((ZN, XN, YN, share_cols, hidden), BF16),
            vm((tok, hidden), BF16),
            vm((hidden, cols), BF16),
            vm((ZN, XN, YN, rows, rank), BF16),
            vm((ZN, XN, YN, rows, rank), BF16),
            vm((rows, rank), F32),
            vm((2, 2, 2, 4, rows, rank // 2), BF16),
            vm((2, 2, 4, rows, rank // 2), BF16),
            vm((2, 2, 2, rows, rank // 2), BF16),
            vm((2, 2, rows, rank // 2), BF16),
            vm((rows, rank), BF16),
        ]
        + small
        + [vm((TN, own, tok), BF16)]
        + dp_sums
        + small
        + dp_sums
        + small
        + [
            vm((TN, own, rank), BF16),
            vm((rank, 2 * rank), F32),
            vm((rank, NB), F32),
            vm((NB, 2 * rank), F32),
            vm((rank, rank), F32),
            vm((rank, rank), F32),
            dma((SEMS,)),
            dma((SEMS,)),
            dma((4,)),
        ],
        compiler_params=pltpu.CompilerParams(
            collective_id=0, has_side_effects=True, vmem_limit_bytes=60 << 20
        ),
    )(probe, activations, gradient)
    correction = lax.dot_general(
        basis.reshape(hidden, rank), wt, (((1,), (1,)), ((), ())), preferred_element_type=F32
    )
    return (gradient.astype(F32) - correction).astype(BF16), gram


def solution(mesh):
    placed = (P("dp", "tensor"), P("tensor", "dp"), P("tensor", "dp"))
    return jax.shard_map(
        local, mesh=mesh, in_specs=placed, out_specs=(P("tensor", "dp"), P()), check_vma=False
    )
```

```python
import jax
import jax.numpy as jnp
from jax import lax
from jax.experimental import pallas as pl
from jax.experimental.pallas import tpu as pltpu
from jax.sharding import PartitionSpec as P

damping_ratio = 0.1
MESH = pl.DeviceIdType.MESH
F32, BF16 = jnp.float32, jnp.bfloat16
HI = lax.Precision.HIGHEST
ZN, XN, YN, TN = 2, 4, 4, 8
NB = 32
AHEAD = 8
SEMS = 210


def dot(a, b, ca, cb, precision=None):
    return lax.dot_general(
        a, b, (((ca,), (cb,)), ((), ())), precision=precision, preferred_element_type=F32
    )


def mod(a, n):
    return lax.rem(a, n)


class Net:
    def __init__(self, send_sem, recv_sem):
        dp, self.t = lax.axis_index("dp"), lax.axis_index("tensor")
        self.z, self.x, self.y = lax.div(dp, XN * YN), mod(lax.div(dp, YN), XN), mod(dp, YN)
        self.send_sem, self.recv_sem, self.count, self.sent = send_sem, recv_sem, 0, []

    def dp(self, z=None, x=None, y=None):
        z, x, y = (own if v is None else v for v, own in ((z, self.z), (x, self.x), (y, self.y)))
        return {"dp": (z * XN + x) * YN + y}

    def step(self, axis, by):
        own, n = (self.x, XN) if axis == "x" else (self.y, YN)
        return self.dp(**{axis: mod(own + by + n, n)})

    def send(self, src, dst, device):
        k = self.count
        self.count += 1
        copy = pltpu.make_async_remote_copy(
            src_ref=src,
            dst_ref=dst,
            send_sem=self.send_sem.at[k],
            recv_sem=self.recv_sem.at[k],
            device_id=device,
            device_id_type=MESH,
        )
        copy.start()
        self.sent.append(copy)
        return copy

    def finish(self):
        assert self.count == SEMS, self.count
        for copy in self.sent:
            copy.wait_send()


def barrier(net):
    sem = pltpu.get_barrier_semaphore()
    peers = [{"tensor": mod(net.t + o, TN)} for o in range(1, TN)]
    peers += [net.step("x", o) for o in range(1, XN)] + [net.step("y", o) for o in range(1, YN)]
    peers += [net.dp(z=1 - net.z)]
    for peer in peers:
        pl.semaphore_signal(sem, inc=1, device_id=peer, device_id_type=MESH)
    pl.semaphore_wait(sem, len(peers))


def gather(net, buf):
    half = buf.shape[-1] // 2
    order = (("x", "y"), ("y", "x"))
    planes = (net.z, 1 - net.z)
    place = {"x": net.x, "y": net.y}
    halves = (0, 1)

    def move(h, ph, plane, i, j, by):
        at = {order[h][0]: mod(place[order[h][0]] + i + 4, 4), order[h][1]: mod(place[order[h][1]] + j + 4, 4)}
        ref = buf.at[planes[plane], at["x"], at["y"], :, pl.ds(h * half, half)]
        return net.send(ref, ref, net.step(order[h][ph], by))

    def both(h, ph, plane, i):
        return move(h, ph, plane, i, 0, 1), move(h, ph, plane, i, 0, -1)

    one = [[None, None], [None, None]]
    two = [[{}, {}], [{}, {}]]
    hop = [[None, None], [None, None]]
    hops = []
    side = (0, 1)

    def launch(plane):
        for h in halves:
            one[plane][h] = both(h, 0, plane, 0)
        for h in halves:
            two[plane][h][0] = both(h, 1, plane, 0)

    def near(plane):
        by = 1 if plane == 0 else -1
        for h in halves:
            for d in (side[plane], 1 - side[plane]):
                one[plane][h][d].wait_recv()
                i = -1 if d == 0 else 1
                if d == side[plane]:
                    hop[plane][h] = move(h, 0, plane, -by, 0, by)
                two[plane][h][i] = both(h, 1, plane, i)

    def far(plane):
        for h in halves:
            hop[plane][h].wait_recv()
            two[plane][h][2] = both(h, 1, plane, 2)

    def onward(plane, i):
        by = 1 if plane == 0 else -1
        for h in halves:
            two[plane][h][i][side[plane]].wait_recv()
            hops.append(move(h, 1, plane, i, -by, by))

    own = buf.at[net.z, net.x, net.y]
    pair = net.send(own, own, net.dp(z=1 - net.z))
    launch(0)
    yield
    near(0)
    yield
    onward(0, 0)
    far(0)
    pair.wait_recv()
    launch(1)
    yield
    onward(0, -1)
    onward(0, 1)
    yield
    near(1)
    onward(0, 2)
    yield
    onward(1, 0)
    far(1)
    yield
    onward(1, -1)
    onward(1, 1)
    yield
    onward(1, 2)
    yield
    for plane in (0, 1):
        for h in halves:
            for i in (0, -1, 1, 2):
                two[plane][h][i][1 - side[plane]].wait_recv()
    for copy in hops:
        copy.wait_recv()
    yield


def add(*refs):
    total = refs[0][...].astype(F32)
    for ref in refs[1:]:
        total = total + ref[...].astype(F32)
    return total


def scatter(net, part, bufs, out, scale):
    order = (("x", "y"), ("y", "x"))
    place = {"x": net.x, "y": net.y}
    half = part.shape[-1] // 2

    def first(h, plane, by):
        a = order[h][0]
        i = mod(place[a] + by + 4, 4)
        lanes = pl.ds(h * half, half)
        return part.at[plane, i, :, :, lanes] if a == "x" else part.at[plane, :, i, :, lanes]

    def second(h, plane, by):
        a = order[h][1]
        i = mod(place[a] + by + 4, 4)
        lanes = pl.ds(h * half, half)
        return part.at[plane, i, net.y, :, lanes] if a == "x" else part.at[plane, net.x, i, :, lanes]

    for ph, block in ((0, first), (1, second)):
        near, far = bufs[2 * ph], bufs[2 * ph + 1]
        s1, s2 = [], []
        for h in (0, 1):
            up, down = net.step(order[h][ph], 1), net.step(order[h][ph], -1)
            s1.append(
                (
                    net.send(block(h, 0, 2), far.at[h, 0], up),
                    net.send(block(h, 1, 2), far.at[h, 1], down),
                )
            )
        yield
        for h in (0, 1):
            up, down = net.step(order[h][ph], 1), net.step(order[h][ph], -1)
            s2.append(
                [
                    net.send(block(h, 1, 1), near.at[h, 0, 1], up),
                    net.send(block(h, 0, -1), near.at[h, 1, 0], down),
                ]
            )
        yield
        for h in (0, 1):
            up, down = net.step(order[h][ph], 1), net.step(order[h][ph], -1)
            s1[h][0].wait_recv()
            ref = block(h, 0, 1)
            ref[...] = add(ref, far.at[h, 0]).astype(BF16)
            s2[h].append(net.send(ref, near.at[h, 0, 0], up))
            s1[h][1].wait_recv()
            ref = block(h, 1, -1)
            ref[...] = add(ref, far.at[h, 1]).astype(BF16)
            s2[h].append(net.send(ref, near.at[h, 1, 1], down))
        yield
        for h in (0, 1):
            for copy in s2[h]:
                copy.wait_recv()
            for plane in (0, 1):
                ref = block(h, plane, 0)
                ref[...] = add(ref, near.at[h, 0, plane], near.at[h, 1, plane]).astype(BF16)
    got = bufs[4]
    last = net.send(part.at[1 - net.z, net.x, net.y], got, net.dp(z=1 - net.z))
    yield
    last.wait_recv()
    out[...] = add(part.at[net.z, net.x, net.y], got) * scale
    yield


def spread(net, part, got):
    copies = []
    for o in range(1, TN):
        peer = mod(net.t + o, TN)
        copies.append(net.send(part.at[peer], got.at[net.t], {"tensor": peer}))
    got[net.t] = part[net.t]
    return copies


def share(net, buf):
    own = buf.at[net.t]
    return [net.send(own, own, {"tensor": mod(net.t + o, TN)}) for o in range(1, TN)]


def landed(copies):
    for copy in copies:
        copy.wait_recv()


def slots(ref):
    total = ref[0].astype(F32)
    for i in range(1, ref.shape[0]):
        total = total + ref[i].astype(F32)
    return total


def dp_sum(net, rows, gy, gx, gz, res):
    gy[net.y] = rows
    copies = [net.send(gy.at[net.y], gy.at[net.y], net.step("y", o)) for o in range(1, YN)]
    yield
    landed(copies)
    gx[net.x] = slots(gy)
    copies = [net.send(gx.at[net.x], gx.at[net.x], net.step("x", o)) for o in range(1, XN)]
    yield
    landed(copies)
    gz[net.z] = slots(gx)
    copy = net.send(gz.at[net.z], gz.at[net.z], net.dp(z=1 - net.z))
    yield
    copy.wait_recv()
    res[net.t] = slots(gz)
    copies = share(net, res)
    yield
    landed(copies)
    yield


def total_sum(net, part, got, gy, gx, gz, res):
    copies = spread(net, part, got)
    yield
    landed(copies)
    yield from dp_sum(net, slots(got), gy, gx, gz, res)


def factor_steps(matrix, work, late, made, inverse):
    n = inverse.shape[0]
    row = lax.broadcasted_iota(jnp.int32, (n, n), 0)
    col = lax.broadcasted_iota(jnp.int32, (n, n), 1)
    work[:, :n] = matrix()
    work[:, n:] = (row == col).astype(F32)
    late[...] = jnp.zeros_like(late)
    made[...] = jnp.zeros_like(made)

    def panel(p, carry):
        r0 = pl.multiple_of(p * NB, NB)
        rows = work[pl.ds(r0, NB), :]
        turned = pltpu.roll(rows[:, :n], mod(n - p * NB, n), 1)[:, :128]
        row = lax.broadcasted_iota(jnp.int32, (NB, 128), 0)
        lane = lax.broadcasted_iota(jnp.int32, (NB, 128), 1)
        block = jnp.where(lane < NB, turned, (lane - NB == row).astype(F32))
        work[...] = work[...] - dot(late[...], made[...], 1, 0, HI)
        columns = [jnp.broadcast_to(block[:, k : k + 1], block.shape) for k in range(AHEAD)]
        for k in range(NB - 1):
            if k + AHEAD < NB:
                columns.append(jnp.broadcast_to(block[:, k + AHEAD : k + AHEAD + 1], block.shape))
            column = columns.pop(0)
            scale = jnp.where(row > k, column * (1.0 / column[k : k + 1, :]), 0.0)
            columns = [later - scale * later[k : k + 1, :] for later in columns]
            block = block - scale * block[k : k + 1, :]
        pivots = jnp.sum(jnp.where(lane == row, block, 0.0), axis=1, keepdims=True)
        block = block / jnp.sqrt(pivots)
        done = dot(block[:, NB : 2 * NB], rows, 1, 0, HI)
        inverse[pl.ds(r0, NB), :] = done[:, n:]
        ahead = lax.broadcasted_iota(jnp.int32, (NB, n), 1) >= r0 + NB
        late[...] = jnp.where(ahead, done[:, :n], 0.0).T
        made[...] = done
        r1 = pl.multiple_of(mod(r0 + NB, n), NB)
        work[pl.ds(r1, NB), :] = work[pl.ds(r1, NB), :] - dot(late[pl.ds(r1, NB), :], done, 1, 0, HI)
        late[pl.ds(r1, NB), :] = jnp.zeros((NB, NB), F32)
        return carry

    for p in range(n // NB):
        lax.fori_loop(p, p + 1, panel, 0)
        yield


def play(order, **tasks):
    for name in order:
        next(tasks[name])


def kernel(
    om_hbm, a_hbm, g_hbm,
    basis_hbm, wt_out, gram_out,
    om, a, g, part, basis, factor,
    near1, far1, near2, far2, pair,
    total, ypart, ygot, ylow,
    cy, cx, cz, core,
    gpart, ggot, gy, gx, gz, gram,
    ppart, pgot, wt,
    work, late, made, linv, kinv,
    send_sem, recv_sem, load_sem,
):
    net = Net(send_sem, recv_sem)
    hidden, rank = basis_hbm.shape[0] * basis_hbm.shape[1] * basis_hbm.shape[2] * basis_hbm.shape[3], basis_hbm.shape[4]
    tok = a.shape[0]
    tokens = tok * ZN * XN * YN
    load_om = pltpu.make_async_copy(om_hbm, om.at[net.z, net.x, net.y], load_sem.at[0])
    load_a = pltpu.make_async_copy(a_hbm, a, load_sem.at[1])
    load_g = pltpu.make_async_copy(g_hbm, g, load_sem.at[2])
    load_om.start()
    load_a.start()
    load_g.start()
    barrier(net)
    load_om.wait()
    for _ in gather(net, om):
        pass
    load_a.wait()

    ck = 512
    total[...] = jnp.zeros_like(total)

    def sketch(i, carry):
        lanes = pl.ds(pl.multiple_of(i * ck, ck), ck)
        probe = om[:, :, :, :, lanes].astype(F32).reshape(rank, ck).astype(BF16)
        total[...] += dot(probe, a[:, lanes], 1, 1)
        return carry

    lax.fori_loop(0, hidden // ck, sketch, 0)
    ypart[...] = total[...].astype(BF16).reshape(ypart.shape)
    landed(spread(net, ypart, ygot))
    yrows = slots(ygot)
    ylow[net.t] = yrows.astype(BF16)
    landed(share(net, ylow))
    low = ylow[...].reshape(rank, tok)
    crows = dot(yrows, low.astype(F32), 1, 1, HI) * (1.0 / tokens)

    def symmetric_core():
        full = core[...].reshape(rank, rank)
        return 0.5 * (full + full.T)

    def core_chain():
        yield from dp_sum(net, crows, cy, cx, cz, core)
        yield from factor_steps(symmetric_core, work, late, made, linv)

    def gram_sum():
        rows = factor[...]
        gpart[...] = dot(rows, rows, 0, 0, HI).reshape(gpart.shape)
        yield from total_sum(net, gpart, ggot, gy, gx, gz, gram)

    def gram_chain():
        half = dot(linv[...], gram[...].reshape(rank, rank), 1, 0, HI)
        full = dot(half, linv[...], 1, 1, HI)
        gram_out[...] = full
        row = lax.broadcasted_iota(jnp.int32, (rank, rank), 0)
        col = lax.broadcasted_iota(jnp.int32, (rank, rank), 1)
        eye = (row == col).astype(F32)
        trace = jnp.sum(jnp.sum(full * eye, axis=1, keepdims=True), axis=0, keepdims=True)
        yield from factor_steps(lambda: full + (damping_ratio / rank) * trace * eye, work, late, made, kinv)

    core_task = core_chain()
    gram_task = gram_sum()
    wide = hidden // 4
    per = wide // part.shape[3]
    low_t = low.T
    next(core_task)
    for c in range(4):
        block = dot(a[:, c * wide : (c + 1) * wide], low_t, 0, 0).astype(BF16)
        part[c // 2, (c % 2) * 2 : (c % 2) * 2 + 2] = block.reshape((per // YN, YN) + part.shape[3:])
    play(
        "rcrrccrrcrcccrccccrgc",
        c=core_task,
        r=scatter(net, part, (near1, far1, near2, far2, pair), factor, 1.0 / tokens),
        g=gram_task,
    )
    local = dot(factor[...], linv[...], 1, 1, HI)
    basis[net.z, net.x, net.y] = local.astype(BF16)
    kernel_task = gram_chain()
    play("gbbgbgbbgbbbb", b=gather(net, basis), g=gram_task)
    store = pltpu.make_async_copy(basis, basis_hbm, load_sem.at[3])
    store.start()
    load_g.wait()
    ppart[...] = jnp.zeros_like(ppart)
    for c in range(4):
        block = basis[c // 2, (c % 2) * 2 : (c % 2) * 2 + 2].reshape(wide, rank)
        ppart[...] += dot(g[c * wide : (c + 1) * wide, :], block, 0, 0).reshape(ppart.shape)
    copies = spread(net, ppart, pgot)
    play("gkkkkkkkk", g=gram_task, k=kernel_task)
    landed(copies)
    solved = dot(dot(slots(pgot), kinv[...], 1, 1, HI), kinv[...], 1, 0, HI)
    wt[net.t] = solved.astype(BF16)
    landed(share(net, wt))
    wt_out[...] = wt[...].reshape(wt_out.shape)
    store.wait()
    net.finish()


def local(activations, test_matrix, gradient):
    tok, hidden = activations.shape
    cols = gradient.shape[1]
    dp = lax.axis_size("dp")
    probe = test_matrix.T
    share_cols = probe.shape[0]
    rank = share_cols * dp
    rows = hidden // dp
    own = rank // TN
    vm, dma = pltpu.VMEM, pltpu.SemaphoreType.DMA
    small = [vm((TN, own, rank), F32), vm((TN, own, rank), F32)]
    dp_sums = [vm((n, own, rank), F32) for n in (YN, XN, ZN, TN)]
    basis, wt, gram = pl.pallas_call(
        kernel,
        out_shape=(
            jax.ShapeDtypeStruct((ZN, XN, YN, rows, rank), BF16),
            jax.ShapeDtypeStruct((cols, rank), BF16),
            jax.ShapeDtypeStruct((rank, rank), F32),
        ),
        in_specs=[pl.BlockSpec(memory_space=pl.ANY)] * 3,
        out_specs=(
            pl.BlockSpec(memory_space=pl.ANY),
            pl.BlockSpec(memory_space=pltpu.VMEM),
            pl.BlockSpec(memory_space=pltpu.VMEM),
        ),
        scratch_shapes=[
            vm((ZN, XN, YN, share_cols, hidden), BF16),
            vm((tok, hidden), BF16),
            vm((hidden, cols), BF16),
            vm((ZN, XN, YN, rows, rank), BF16),
            vm((ZN, XN, YN, rows, rank), BF16),
            vm((rows, rank), F32),
            vm((2, 2, 2, 4, rows, rank // 2), BF16),
            vm((2, 2, 4, rows, rank // 2), BF16),
            vm((2, 2, 2, rows, rank // 2), BF16),
            vm((2, 2, rows, rank // 2), BF16),
            vm((rows, rank), BF16),
        ]
        + [vm((rank, tok), F32)]
        + [vm((TN, own, tok), BF16)] * 3
        + dp_sums
        + small
        + dp_sums
        + small
        + [
            vm((TN, own, rank), BF16),
            vm((rank, 2 * rank), F32),
            vm((rank, NB), F32),
            vm((NB, 2 * rank), F32),
            vm((rank, rank), F32),
            vm((rank, rank), F32),
            dma((SEMS,)),
            dma((SEMS,)),
            dma((4,)),
        ],
        compiler_params=pltpu.CompilerParams(
            collective_id=0, has_side_effects=True, vmem_limit_bytes=60 << 20
        ),
    )(probe, activations, gradient)
    correction = lax.dot_general(
        basis.reshape(hidden, rank), wt, (((1,), (1,)), ((), ())), preferred_element_type=F32
    )
    return (gradient.astype(F32) - correction).astype(BF16), gram


def solution(mesh):
    placed = (P("dp", "tensor"), P("tensor", "dp"), P("tensor", "dp"))
    return jax.shard_map(
        local, mesh=mesh, in_specs=placed, out_specs=(P("tensor", "dp"), P()), check_vma=False
    )
```

```python
import jax
import jax.numpy as jnp
from jax import lax
from jax.experimental import pallas as pl
from jax.experimental.pallas import tpu as pltpu
from jax.sharding import PartitionSpec as P

damping_ratio = 0.1
MESH = pl.DeviceIdType.MESH
F32, BF16 = jnp.float32, jnp.bfloat16
HI = lax.Precision.HIGHEST
ZN, XN, YN, TN = 2, 4, 4, 8
NB = 32
AHEAD = 8
SEMS = 210


def dot(a, b, ca, cb, precision=None):
    return lax.dot_general(
        a, b, (((ca,), (cb,)), ((), ())), precision=precision, preferred_element_type=F32
    )


def mod(a, n):
    return lax.rem(a, n)


class Net:
    def __init__(self, send_sem, recv_sem):
        dp, self.t = lax.axis_index("dp"), lax.axis_index("tensor")
        self.z, self.x, self.y = lax.div(dp, XN * YN), mod(lax.div(dp, YN), XN), mod(dp, YN)
        self.send_sem, self.recv_sem, self.count, self.sent = send_sem, recv_sem, 0, []

    def dp(self, z=None, x=None, y=None):
        z, x, y = (own if v is None else v for v, own in ((z, self.z), (x, self.x), (y, self.y)))
        return {"dp": (z * XN + x) * YN + y}

    def step(self, axis, by):
        own, n = (self.x, XN) if axis == "x" else (self.y, YN)
        return self.dp(**{axis: mod(own + by + n, n)})

    def send(self, src, dst, device):
        k = self.count
        self.count += 1
        copy = pltpu.make_async_remote_copy(
            src_ref=src,
            dst_ref=dst,
            send_sem=self.send_sem.at[k],
            recv_sem=self.recv_sem.at[k],
            device_id=device,
            device_id_type=MESH,
        )
        copy.start()
        self.sent.append(copy)
        return copy

    def finish(self):
        assert self.count == SEMS, self.count
        for copy in self.sent:
            copy.wait_send()


def barrier(net):
    sem = pltpu.get_barrier_semaphore()
    peers = [{"tensor": mod(net.t + o, TN)} for o in range(1, TN)]
    peers += [net.step("x", o) for o in range(1, XN)] + [net.step("y", o) for o in range(1, YN)]
    peers += [net.dp(z=1 - net.z)]
    for peer in peers:
        pl.semaphore_signal(sem, inc=1, device_id=peer, device_id_type=MESH)
    pl.semaphore_wait(sem, len(peers))


def gather(net, buf):
    half = buf.shape[-1] // 2
    order = (("x", "y"), ("y", "x"))
    planes = (net.z, 1 - net.z)
    place = {"x": net.x, "y": net.y}
    halves = (0, 1)

    def move(h, ph, plane, i, j, by):
        at = {order[h][0]: mod(place[order[h][0]] + i + 4, 4), order[h][1]: mod(place[order[h][1]] + j + 4, 4)}
        ref = buf.at[planes[plane], at["x"], at["y"], :, pl.ds(h * half, half)]
        return net.send(ref, ref, net.step(order[h][ph], by))

    def both(h, ph, plane, i):
        return move(h, ph, plane, i, 0, 1), move(h, ph, plane, i, 0, -1)

    one = [[None, None], [None, None]]
    two = [[{}, {}], [{}, {}]]
    hop = [[None, None], [None, None]]
    hops = []
    side = (0, 1)

    def launch(plane):
        for h in halves:
            one[plane][h] = both(h, 0, plane, 0)
        for h in halves:
            two[plane][h][0] = both(h, 1, plane, 0)

    def near(plane):
        by = 1 if plane == 0 else -1
        for h in halves:
            for d in (side[plane], 1 - side[plane]):
                one[plane][h][d].wait_recv()
                i = -1 if d == 0 else 1
                if d == side[plane]:
                    hop[plane][h] = move(h, 0, plane, -by, 0, by)
                two[plane][h][i] = both(h, 1, plane, i)

    def far(plane):
        for h in halves:
            hop[plane][h].wait_recv()
            two[plane][h][2] = both(h, 1, plane, 2)

    def onward(plane, i):
        by = 1 if plane == 0 else -1
        for h in halves:
            two[plane][h][i][side[plane]].wait_recv()
            hops.append(move(h, 1, plane, i, -by, by))

    own = buf.at[net.z, net.x, net.y]
    pair = net.send(own, own, net.dp(z=1 - net.z))
    launch(0)
    yield
    near(0)
    yield
    onward(0, 0)
    far(0)
    pair.wait_recv()
    launch(1)
    yield
    onward(0, -1)
    onward(0, 1)
    yield
    near(1)
    onward(0, 2)
    yield
    onward(1, 0)
    far(1)
    yield
    onward(1, -1)
    onward(1, 1)
    yield
    onward(1, 2)
    yield
    for plane in (0, 1):
        for h in halves:
            for i in (0, -1, 1, 2):
                two[plane][h][i][1 - side[plane]].wait_recv()
    for copy in hops:
        copy.wait_recv()
    yield


def add(*refs):
    total = refs[0][...].astype(F32)
    for ref in refs[1:]:
        total = total + ref[...].astype(F32)
    return total


def scatter(net, part, bufs, out, scale):
    order = (("x", "y"), ("y", "x"))
    place = {"x": net.x, "y": net.y}
    half = part.shape[-1] // 2

    def first(h, plane, by):
        a = order[h][0]
        i = mod(place[a] + by + 4, 4)
        lanes = pl.ds(h * half, half)
        return part.at[plane, i, :, :, lanes] if a == "x" else part.at[plane, :, i, :, lanes]

    def second(h, plane, by):
        a = order[h][1]
        i = mod(place[a] + by + 4, 4)
        lanes = pl.ds(h * half, half)
        return part.at[plane, i, net.y, :, lanes] if a == "x" else part.at[plane, net.x, i, :, lanes]

    for ph, block in ((0, first), (1, second)):
        near, far = bufs[2 * ph], bufs[2 * ph + 1]
        s1, s2 = [], []
        for h in (0, 1):
            up, down = net.step(order[h][ph], 1), net.step(order[h][ph], -1)
            s1.append(
                (
                    net.send(block(h, 0, 2), far.at[h, 0], up),
                    net.send(block(h, 1, 2), far.at[h, 1], down),
                )
            )
        yield
        for h in (0, 1):
            up, down = net.step(order[h][ph], 1), net.step(order[h][ph], -1)
            s2.append(
                [
                    net.send(block(h, 1, 1), near.at[h, 0, 1], up),
                    net.send(block(h, 0, -1), near.at[h, 1, 0], down),
                ]
            )
        yield
        for h in (0, 1):
            up, down = net.step(order[h][ph], 1), net.step(order[h][ph], -1)
            s1[h][0].wait_recv()
            ref = block(h, 0, 1)
            ref[...] = add(ref, far.at[h, 0]).astype(BF16)
            s2[h].append(net.send(ref, near.at[h, 0, 0], up))
            s1[h][1].wait_recv()
            ref = block(h, 1, -1)
            ref[...] = add(ref, far.at[h, 1]).astype(BF16)
            s2[h].append(net.send(ref, near.at[h, 1, 1], down))
        yield
        for h in (0, 1):
            for copy in s2[h]:
                copy.wait_recv()
            for plane in (0, 1):
                ref = block(h, plane, 0)
                ref[...] = add(ref, near.at[h, 0, plane], near.at[h, 1, plane]).astype(BF16)
    got = bufs[4]
    last = net.send(part.at[1 - net.z, net.x, net.y], got, net.dp(z=1 - net.z))
    yield
    last.wait_recv()
    out[...] = add(part.at[net.z, net.x, net.y], got) * scale
    yield


def spread(net, part, got):
    copies = []
    for o in range(1, TN):
        peer = mod(net.t + o, TN)
        copies.append(net.send(part.at[peer], got.at[net.t], {"tensor": peer}))
    got[net.t] = part[net.t]
    return copies


def share(net, buf):
    own = buf.at[net.t]
    return [net.send(own, own, {"tensor": mod(net.t + o, TN)}) for o in range(1, TN)]


def landed(copies):
    for copy in copies:
        copy.wait_recv()


def slots(ref):
    total = ref[0].astype(F32)
    for i in range(1, ref.shape[0]):
        total = total + ref[i].astype(F32)
    return total


def dp_sum(net, rows, gy, gx, gz, res):
    gy[net.y] = rows
    copies = [net.send(gy.at[net.y], gy.at[net.y], net.step("y", o)) for o in range(1, YN)]
    yield
    landed(copies)
    gx[net.x] = slots(gy)
    copies = [net.send(gx.at[net.x], gx.at[net.x], net.step("x", o)) for o in range(1, XN)]
    yield
    landed(copies)
    gz[net.z] = slots(gx)
    copy = net.send(gz.at[net.z], gz.at[net.z], net.dp(z=1 - net.z))
    yield
    copy.wait_recv()
    res[net.t] = slots(gz)
    copies = share(net, res)
    yield
    landed(copies)
    yield


def total_sum(net, part, got, gy, gx, gz, res):
    copies = spread(net, part, got)
    yield
    landed(copies)
    yield from dp_sum(net, slots(got), gy, gx, gz, res)


def factor_steps(matrix, work, late, made, inverse):
    n = inverse.shape[0]
    row = lax.broadcasted_iota(jnp.int32, (n, n), 0)
    col = lax.broadcasted_iota(jnp.int32, (n, n), 1)
    work[:, :n] = matrix()
    work[:, n:] = (row == col).astype(F32)
    late[...] = jnp.zeros_like(late)
    made[...] = jnp.zeros_like(made)

    def panel(p, carry):
        r0 = pl.multiple_of(p * NB, NB)
        rows = work[pl.ds(r0, NB), :]
        turned = pltpu.roll(rows[:, :n], mod(n - p * NB, n), 1)[:, :128]
        row = lax.broadcasted_iota(jnp.int32, (NB, 128), 0)
        lane = lax.broadcasted_iota(jnp.int32, (NB, 128), 1)
        block = jnp.where(lane < NB, turned, (lane - NB == row).astype(F32))
        work[...] = work[...] - dot(late[...], made[...], 1, 0, HI)
        columns = [jnp.broadcast_to(block[:, k : k + 1], block.shape) for k in range(AHEAD)]
        for k in range(NB - 1):
            if k + AHEAD < NB:
                columns.append(jnp.broadcast_to(block[:, k + AHEAD : k + AHEAD + 1], block.shape))
            column = columns.pop(0)
            scale = jnp.where(row > k, column * (1.0 / column[k : k + 1, :]), 0.0)
            columns = [later - scale * later[k : k + 1, :] for later in columns]
            block = block - scale * block[k : k + 1, :]
        pivots = jnp.sum(jnp.where(lane == row, block, 0.0), axis=1, keepdims=True)
        block = block / jnp.sqrt(pivots)
        done = dot(block[:, NB : 2 * NB], rows, 1, 0, HI)
        inverse[pl.ds(r0, NB), :] = done[:, n:]
        ahead = lax.broadcasted_iota(jnp.int32, (NB, n), 1) >= r0 + NB
        late[...] = jnp.where(ahead, done[:, :n], 0.0).T
        made[...] = done
        r1 = pl.multiple_of(mod(r0 + NB, n), NB)
        work[pl.ds(r1, NB), :] = work[pl.ds(r1, NB), :] - dot(late[pl.ds(r1, NB), :], done, 1, 0, HI)
        late[pl.ds(r1, NB), :] = jnp.zeros((NB, NB), F32)
        return carry

    for p in range(n // NB):
        lax.fori_loop(p, p + 1, panel, 0)
        yield


def play(order, **tasks):
    for name in order:
        next(tasks[name])


def kernel(
    om_hbm, a_hbm, g_hbm,
    basis_hbm, wt_out, gram_out,
    om, a, g, part, basis, factor,
    near1, far1, near2, far2, pair,
    total, ypart, ygot, ylow,
    cy, cx, cz, core,
    gpart, ggot, gy, gx, gz, gram,
    ppart, pgot, wt,
    work, late, made, linv, kinv,
    send_sem, recv_sem, load_sem,
):
    net = Net(send_sem, recv_sem)
    hidden, rank = basis_hbm.shape[0] * basis_hbm.shape[1] * basis_hbm.shape[2] * basis_hbm.shape[3], basis_hbm.shape[4]
    tok = a.shape[0]
    tokens = tok * ZN * XN * YN
    load_om = pltpu.make_async_copy(om_hbm, om.at[net.z, net.x, net.y], load_sem.at[0])
    load_a = pltpu.make_async_copy(a_hbm, a, load_sem.at[1])
    load_g = pltpu.make_async_copy(g_hbm, g, load_sem.at[2])
    load_om.start()
    load_a.start()
    load_g.start()
    barrier(net)
    load_om.wait()
    for _ in gather(net, om):
        pass
    load_a.wait()

    ck = 1664
    total[...] = jnp.zeros_like(total)

    def sketch(i, carry):
        lanes = pl.ds(pl.multiple_of(i * ck, ck), ck)
        probe = om[:, :, :, :, lanes].astype(F32).reshape(rank, ck).astype(BF16)
        total[...] += dot(probe, a[:, lanes], 1, 1)
        return carry

    lax.fori_loop(0, hidden // ck, sketch, 0)
    ypart[...] = total[...].astype(BF16).reshape(ypart.shape)
    landed(spread(net, ypart, ygot))
    yrows = slots(ygot)
    ylow[net.t] = yrows.astype(BF16)
    landed(share(net, ylow))
    low = ylow[...].reshape(rank, tok)
    crows = dot(yrows, low.astype(F32), 1, 1, HI) * (1.0 / tokens)

    def symmetric_core():
        full = core[...].reshape(rank, rank)
        return 0.5 * (full + full.T)

    def core_chain():
        yield from dp_sum(net, crows, cy, cx, cz, core)
        yield from factor_steps(symmetric_core, work, late, made, linv)

    def gram_sum():
        rows = factor[...]
        gpart[...] = dot(rows, rows, 0, 0, HI).reshape(gpart.shape)
        yield from total_sum(net, gpart, ggot, gy, gx, gz, gram)

    def gram_chain():
        half = dot(linv[...], gram[...].reshape(rank, rank), 1, 0, HI)
        full = dot(half, linv[...], 1, 1, HI)
        gram_out[...] = full
        row = lax.broadcasted_iota(jnp.int32, (rank, rank), 0)
        col = lax.broadcasted_iota(jnp.int32, (rank, rank), 1)
        eye = (row == col).astype(F32)
        trace = jnp.sum(jnp.sum(full * eye, axis=1, keepdims=True), axis=0, keepdims=True)
        yield from factor_steps(lambda: full + (damping_ratio / rank) * trace * eye, work, late, made, kinv)

    core_task = core_chain()
    gram_task = gram_sum()
    wide = hidden // 4
    per = wide // part.shape[3]
    low_t = low.T
    next(core_task)
    for c in range(4):
        block = dot(a[:, c * wide : (c + 1) * wide], low_t, 0, 0).astype(BF16)
        part[c // 2, (c % 2) * 2 : (c % 2) * 2 + 2] = block.reshape((per // YN, YN) + part.shape[3:])
    play(
        "rcrrccrrcrcccrccccrgc",
        c=core_task,
        r=scatter(net, part, (near1, far1, near2, far2, pair), factor, 1.0 / tokens),
        g=gram_task,
    )
    local = dot(factor[...], linv[...], 1, 1, HI)
    basis[net.z, net.x, net.y] = local.astype(BF16)
    kernel_task = gram_chain()
    play("gbbgbgbbgbbbb", b=gather(net, basis), g=gram_task)
    store = pltpu.make_async_copy(basis, basis_hbm, load_sem.at[3])
    store.start()
    load_g.wait()
    ppart[...] = jnp.zeros_like(ppart)
    for c in range(4):
        block = basis[c // 2, (c % 2) * 2 : (c % 2) * 2 + 2].reshape(wide, rank)
        ppart[...] += dot(g[c * wide : (c + 1) * wide, :], block, 0, 0).reshape(ppart.shape)
    copies = spread(net, ppart, pgot)
    play("gkkkkkkkk", g=gram_task, k=kernel_task)
    landed(copies)
    solved = dot(dot(slots(pgot), kinv[...], 1, 1, HI), kinv[...], 1, 0, HI)
    wt[net.t] = solved.astype(BF16)
    landed(share(net, wt))
    wt_out[...] = wt[...].reshape(wt_out.shape)
    store.wait()
    net.finish()


def local(activations, test_matrix, gradient):
    tok, hidden = activations.shape
    cols = gradient.shape[1]
    dp = lax.axis_size("dp")
    probe = test_matrix.T
    share_cols = probe.shape[0]
    rank = share_cols * dp
    rows = hidden // dp
    own = rank // TN
    vm, dma = pltpu.VMEM, pltpu.SemaphoreType.DMA
    small = [vm((TN, own, rank), F32), vm((TN, own, rank), F32)]
    dp_sums = [vm((n, own, rank), F32) for n in (YN, XN, ZN, TN)]
    basis, wt, gram = pl.pallas_call(
        kernel,
        out_shape=(
            jax.ShapeDtypeStruct((ZN, XN, YN, rows, rank), BF16),
            jax.ShapeDtypeStruct((cols, rank), BF16),
            jax.ShapeDtypeStruct((rank, rank), F32),
        ),
        in_specs=[pl.BlockSpec(memory_space=pl.ANY)] * 3,
        out_specs=(
            pl.BlockSpec(memory_space=pl.ANY),
            pl.BlockSpec(memory_space=pltpu.VMEM),
            pl.BlockSpec(memory_space=pltpu.VMEM),
        ),
        scratch_shapes=[
            vm((ZN, XN, YN, share_cols, hidden), BF16),
            vm((tok, hidden), BF16),
            vm((hidden, cols), BF16),
            vm((ZN, XN, YN, rows, rank), BF16),
            vm((ZN, XN, YN, rows, rank), BF16),
            vm((rows, rank), F32),
            vm((2, 2, 2, 4, rows, rank // 2), BF16),
            vm((2, 2, 4, rows, rank // 2), BF16),
            vm((2, 2, 2, rows, rank // 2), BF16),
            vm((2, 2, rows, rank // 2), BF16),
            vm((rows, rank), BF16),
        ]
        + [vm((rank, tok), F32)]
        + [vm((TN, own, tok), BF16)] * 3
        + dp_sums
        + small
        + dp_sums
        + small
        + [
            vm((TN, own, rank), BF16),
            vm((rank, 2 * rank), F32),
            vm((rank, NB), F32),
            vm((NB, 2 * rank), F32),
            vm((rank, rank), F32),
            vm((rank, rank), F32),
            dma((SEMS,)),
            dma((SEMS,)),
            dma((4,)),
        ],
        compiler_params=pltpu.CompilerParams(
            collective_id=0, has_side_effects=True, vmem_limit_bytes=60 << 20
        ),
    )(probe, activations, gradient)
    correction = lax.dot_general(
        basis.reshape(hidden, rank), wt, (((1,), (1,)), ((), ())), preferred_element_type=F32
    )
    return (gradient.astype(F32) - correction).astype(BF16), gram


def solution(mesh):
    placed = (P("dp", "tensor"), P("tensor", "dp"), P("tensor", "dp"))
    return jax.shard_map(
        local, mesh=mesh, in_specs=placed, out_specs=(P("tensor", "dp"), P()), check_vma=False
    )
```
